32 devices in a mesh: groups: 2 (over x), tiles: 16 (over z, y, core).
Axes of the slice: x: 2, y: 2, z: 4, core: 2. Of those that a mesh axis runs over, the one named last changes fastest.
Arguments:
- tiles: bfloat16 [3, 8192], P(None, ('groups', 'tiles')), parts along dimension 1, may hold values from 0 to 1
- tile_slide: int32 [128], P(('groups', 'tiles')), parts along dimension 0, may hold values from 0 to 383
- tile_mask: int32 [128], P(('groups', 'tiles')), parts along dimension 0, may hold values from 0 to 1, as said below
- tile_label: int32 [128], P(('groups', 'tiles')), parts along dimension 0, may hold values from 0 to 8
- attack_field: float32 [49152], P(('groups', 'tiles')), parts along dimension 0, may hold values from -1 to 1
- lift_weight: float32 [9, 3, 128], replicated, may hold values from -1.25 to 1.25
- group_weight: bfloat16 [8, 9, 128, 128], replicated, may hold values from -0.0625 to 0.0625
- class_weight: float32 [128, 9], replicated, may hold values from -0.5 to 0.5
Outputs:
- margins: float32 [128], P(('groups', 'tiles')), parts along dimension 0
- attack_grad: float32 [49152], P(('groups', 'tiles')), parts along dimension 0
The draws below stay inside these ranges and needn't reach their ends.
There are 2 independent parts, one for each index of `groups`. The reference program is written for one: setup_inputs(seed, part) draws one part's arguments, and reference() takes and returns one part's arrays. A program takes and returns all parts, laid end to end along the dimension named above; an argument that names none is the same for every part. Nothing has to cross between parts.
Inputs may be any that keep to these rules, and one draw needn't show every extreme that they name: `tile_mask`: in every part the live tiles number exactly 2 times the devices of the tiles axis in all; one device holds 0 to 4 of them, and on some device all 4 slots are live.
All inputs are finite; a program needn't handle non-finite values.
Results may differ from the reference program's by a relative error of at most 0.007.
Values may be sent and summed in bfloat16 or wider, within the bound.
A program may use at most 128 MiB of HBM per device.

```python
import math
import jax
import jax.numpy as jnp
import numpy as np
from jax import lax

HUES = 8
CH = 128
CLASSES = 9
TILE = 8
PIX = 64
BAL = 2
CAP = 4
SLIDES = 384
TOTAL_SLOTS = 64
N_TILES = 16


def draw_tile_mask(key, part):
    base_key = jax.random.fold_in(key, 101)
    key_list = jax.random.split(base_key, 4)
    device_order = jax.random.permutation(key_list[0], N_TILES)
    shift_amount = jax.random.randint(key_list[1], (N_TILES // 2,), -BAL, BAL + 1)
    chosen_pair = jax.random.randint(key_list[2], (), 0, N_TILES // 2)
    shift_amount = jnp.where(jnp.arange(N_TILES // 2) == chosen_pair, BAL, shift_amount)
    pair_loads = jnp.stack([BAL + shift_amount, BAL - shift_amount], axis=1).reshape(N_TILES)
    tile_loads = jnp.zeros((N_TILES,), jnp.int32).at[device_order].set(pair_loads.astype(jnp.int32))
    priority = jax.vmap(lambda device_key: jax.random.permutation(device_key, CAP))(jax.random.split(key_list[3], N_TILES))
    live_mask = (priority < tile_loads[:, None]).astype(jnp.int32)
    return live_mask.reshape(N_TILES * CAP)


def set_ends(values, stream_key, least, largest):
    dims = values.shape
    spot = [jax.random.randint(jax.random.fold_in(stream_key, axis), (), 0, dims[axis]) for axis in range(len(dims))]
    values = values.at[tuple(spot)].set(least)
    longest = dims.index(max(dims))
    spot[longest] = (spot[longest] + 1) % dims[longest]
    return values.at[tuple(spot)].set(largest)


def shard_levels(own_key, dims, cuts, low, top_value):
    gain = 1.0
    for position, parts in cuts:
        heights = jax.random.uniform(jax.random.fold_in(jax.random.fold_in(own_key, 6), position), (parts,), jnp.float32, low / len(cuts), top_value / len(cuts))
        gain = gain * jnp.repeat(jnp.exp(heights), dims[position] // parts).reshape((-1,) + (1,) * (len(dims) - 1 - position))
    return gain


def gaussian(key, extent, spread, reach, kind=jnp.bfloat16):
    values = jax.random.normal(key, extent, jnp.float32) * spread
    return jnp.minimum(jnp.maximum(values, -reach), reach).astype(kind)


def setup_inputs(seed: int = 0, part: int = 0) -> dict:
    keys = jax.random.split(jax.random.key(seed), 9)
    part_splits = jax.random.split(jax.random.fold_in(keys[8], part), 9)
    return {
        "tiles": jnp.clip(1.0 * jax.random.uniform(part_splits[0], (3, TOTAL_SLOTS * PIX), jnp.float32) ** shard_levels(part_splits[0], (3, TOTAL_SLOTS * PIX), ((1, 16),), -0.2, 0.2), 0.0, 1.0).astype(jnp.bfloat16),
        "tile_slide": set_ends(jax.random.randint(part_splits[1], (TOTAL_SLOTS,), 0, SLIDES), jax.random.fold_in(part_splits[1], 1), 0, SLIDES - 1).astype(jnp.int32),
        "tile_mask": draw_tile_mask(jax.random.fold_in(jax.random.fold_in(keys[8], part), 71), part),
        "tile_label": set_ends(jax.random.randint(part_splits[3], (TOTAL_SLOTS,), 0, CLASSES), jax.random.fold_in(part_splits[3], 1), 0, CLASSES - 1).astype(jnp.int32),
        "attack_field": jnp.clip(jax.random.uniform(part_splits[4], (SLIDES * PIX,), jnp.float32, -1.0, 1.0) * shard_levels(part_splits[4], (SLIDES * PIX,), ((0, 16),), -0.4, 0.0), -1.0, 1.0),
        "lift_weight": gaussian(keys[5], (9, 3, CH), 27 ** -0.5, 1.25, jnp.float32),
        "group_weight": gaussian(keys[6], (HUES, 9, CH, CH), (9 * HUES * CH) ** -0.5, 0.0625),
        "class_weight": gaussian(keys[7], (CH, CLASSES), CH ** -0.5, 0.5, jnp.float32),
    }


def hue_rotations(hue_count):
    factor = 1.0 / math.sqrt(3.0)
    skew_part = factor * np.array([[0.0, -1.0, 1.0], [1.0, 0.0, -1.0], [-1.0, 1.0, 0.0]])
    result = []
    for number in range(hue_count):
        rotation_angle = -2.0 * math.pi * number / hue_count
        result.append(math.cos(rotation_angle) * np.eye(3) + math.sin(rotation_angle) * skew_part + (1.0 - math.cos(rotation_angle)) * np.ones((3, 3)) / 3.0)
    return np.stack(result)

def lift_matrix(lift_weight, hue_count):
    rotations = jnp.asarray(hue_rotations(hue_count), dtype=jnp.float32)
    mapped = jnp.einsum('tio,kij->tjko', lift_weight.astype(jnp.float32), rotations, precision=lax.Precision.HIGHEST)
    return mapped.reshape(27, hue_count * lift_weight.shape[2])

def circulant(group_weight, tap_index):
    hue_count = group_weight.shape[0]
    channels = group_weight.shape[2]
    index_table = np.array([[(source - target) % hue_count for target in range(hue_count)] for source in range(hue_count)], dtype=np.int32)
    blocks = group_weight[:, tap_index][index_table]
    return blocks.transpose(0, 2, 1, 3).reshape(hue_count * channels, hue_count * channels)

def grey_cross(colours):
    factor = 1.0 / math.sqrt(3.0)
    red_part = colours[:, 0]
    green_part = colours[:, 1]
    blue_part = colours[:, 2]
    return factor * jnp.stack([blue_part - green_part, red_part - blue_part, green_part - red_part], axis=1)

def neighbours(feature, tap_index, forward):
    tile_side = feature.shape[1]
    padded = jnp.pad(feature, ((0, 0), (1, 1), (1, 1), (0, 0)))
    row_start = tap_index // 3
    column_start = tap_index % 3
    if not forward:
        row_start = 2 - row_start
        column_start = 2 - column_start
    return padded[:, row_start:row_start + tile_side, column_start:column_start + tile_side]

def silu_slope(values):
    logistic = jax.nn.sigmoid(values)
    return logistic * (1.0 + values * (1.0 - logistic))

def tile_attack(pixels, angles, score_grad, lifting, circulants, class_weight):
    slot_count = pixels.shape[0]
    channels = class_weight.shape[0]
    width = circulants.shape[1]
    hue_count = width // channels
    tile_side = TILE
    pixel_count = tile_side * tile_side
    colours = pixels.astype(jnp.float32)
    cos_angle = jnp.cos(angles)[:, None, :]
    sin_angle = jnp.sin(angles)[:, None, :]
    cross_term = grey_cross(colours)
    grey_level = lax.optimization_barrier(jnp.mean(colours, axis=1, keepdims=True))
    attacked = cos_angle * colours + sin_angle * cross_term + (1.0 - cos_angle) * grey_level
    picture = attacked.reshape(slot_count, 3, tile_side, tile_side).transpose(0, 2, 3, 1)
    patches = jnp.concatenate([neighbours(picture, tap_index, True) for tap_index in range(9)], axis=3)
    patches = patches.reshape(slot_count * pixel_count, 27)
    lifted = jnp.dot(patches, lifting, precision=lax.Precision.HIGHEST, preferred_element_type=jnp.float32)
    activated = jax.nn.silu(lifted).astype(jnp.bfloat16).reshape(slot_count, tile_side, tile_side, width)
    mixed = jnp.zeros((slot_count * pixel_count, width), jnp.float32)
    for tap_index in range(9):
        shifted = neighbours(activated, tap_index, True).reshape(slot_count * pixel_count, width)
        mixed = mixed + jnp.dot(shifted, circulants[tap_index], preferred_element_type=jnp.float32)
    pooled = lax.optimization_barrier(jnp.mean(jax.nn.silu(mixed).reshape(slot_count, pixel_count * hue_count, channels), axis=1))
    scores = jnp.dot(pooled, class_weight, precision=lax.Precision.HIGHEST, preferred_element_type=jnp.float32)
    margins = -lax.optimization_barrier(jnp.sum(score_grad * scores, axis=1)) / pixel_count
    pooled_grad = lax.dot_general(score_grad, class_weight, (((1,), (1,)), ((), ())), precision=lax.Precision.HIGHEST, preferred_element_type=jnp.float32)
    spread_grad = jnp.broadcast_to((pooled_grad / (hue_count * pixel_count))[:, None, :], (slot_count, pixel_count * hue_count, channels))
    spread_grad = spread_grad.reshape(slot_count * pixel_count, width)
    mixed_grad = (spread_grad * silu_slope(mixed)).astype(jnp.bfloat16)
    mixed_grad = mixed_grad.reshape(slot_count, tile_side, tile_side, width)
    act_grad = jnp.zeros((slot_count * pixel_count, width), jnp.float32)
    for tap_index in range(9):
        shifted = neighbours(mixed_grad, tap_index, False).reshape(slot_count * pixel_count, width)
        act_grad = act_grad + lax.dot_general(shifted, circulants[tap_index], (((1,), (1,)), ((), ())), preferred_element_type=jnp.float32)
    lifted_grad = act_grad * silu_slope(lifted)
    patch_grad = lax.dot_general(lifted_grad, lifting, (((1,), (1,)), ((), ())), precision=lax.Precision.HIGHEST, preferred_element_type=jnp.float32)
    patch_grad = patch_grad.reshape(slot_count, tile_side, tile_side, 9, 3)
    picture_grad = jnp.zeros((slot_count, tile_side, tile_side, 3), jnp.float32)
    for tap_index in range(9):
        picture_grad = picture_grad + neighbours(patch_grad[:, :, :, tap_index, :], tap_index, False)
    colour_grad = picture_grad.transpose(0, 3, 1, 2).reshape(slot_count, 3, pixel_count)
    turning = -sin_angle * colours + cos_angle * cross_term + sin_angle * grey_level
    angle_grad = lax.optimization_barrier(jnp.sum(colour_grad * turning, axis=1))
    return (angle_grad, margins)

def reference(tiles, tile_slide, tile_mask, tile_label, attack_field, lift_weight, group_weight, class_weight):
    live_total = N_TILES * BAL
    picked = jnp.nonzero(tile_mask, size=live_total)[0].astype(jnp.int32)
    pixels = tiles.reshape(3, TOTAL_SLOTS, PIX).transpose(1, 0, 2)[picked]
    slides = tile_slide[picked]
    classes = class_weight.shape[1]
    label_hot = (tile_label[picked][:, None] == jnp.arange(classes, dtype=jnp.int32)[None, :]).astype(jnp.float32)
    score_grad = PIX * (1.0 / classes - label_hot)
    angles = attack_field.reshape(SLIDES, PIX)[slides]
    lifting = lift_matrix(lift_weight, group_weight.shape[0])
    circulants = jnp.stack([circulant(group_weight, tap_index) for tap_index in range(9)])
    block_total = N_TILES // 8

    def attack_block(inputs):
        return tile_attack(inputs[0], inputs[1], inputs[2], lifting, circulants, class_weight)
    angle_grad, margins_live = lax.map(attack_block, (pixels.reshape(block_total, 8 * BAL, 3, PIX), angles.reshape(block_total, 8 * BAL, PIX), score_grad.reshape(block_total, 8 * BAL, classes)))
    angle_grad = angle_grad.reshape(live_total, PIX)
    margins_live = margins_live.reshape(live_total)
    raw_sums = jax.ops.segment_sum(angle_grad, slides, num_segments=SLIDES)
    counts = jax.ops.segment_sum(jnp.ones((live_total,), jnp.float32), slides, num_segments=SLIDES)
    attack_grad = (raw_sums / jnp.maximum(counts, 1.0)[:, None]).reshape(SLIDES * PIX)
    margins = jnp.zeros((TOTAL_SLOTS,), jnp.float32).at[picked].set(margins_live)
    return (margins, attack_grad)
```

```python
import functools
import math

import jax
import jax.numpy as jnp
from jax import lax
from jax.experimental import pallas as pl
from jax.experimental.pallas import tpu as pltpu
from jax.sharding import PartitionSpec as P

F32 = jnp.float32
BF16 = jnp.bfloat16
HIGHEST = lax.Precision.HIGHEST
ROOT_HALF = math.sqrt(0.5)
CROSS = 1.0 / math.sqrt(3.0)
PIX = 64
LANES = 128
TAPS = [(tap // 3 - 1, tap % 3 - 1) for tap in range(9)]


def hue_transform(x):
    s04, d04 = x[0] + x[4], x[0] - x[4]
    s15, d15 = x[1] + x[5], x[1] - x[5]
    s26, d26 = x[2] + x[6], x[2] - x[6]
    s37, d37 = x[3] + x[7], x[3] - x[7]
    even, odd = s04 + s26, s15 + s37
    dc = ROOT_HALF * (d15 - d37)
    ds = ROOT_HALF * (d15 + d37)
    return [
        (even + odd, even - odd),
        (d04 + dc, d26 + ds),
        (s04 - s26, s15 - s37),
        (d04 - dc, ds - d26),
    ]


def hue_spread(parts):
    (c0, c4), (a1, b1), (a2, b2), (a3, b3) = parts
    e0, e1 = c0 + c4, c0 - c4
    u0, u1 = e0 + a2, a1 + a3
    w0, w1 = e0 - a2, b1 - b3
    da = ROOT_HALF * (a1 - a3)
    db = ROOT_HALF * (b1 + b3)
    p1, q1 = e1 + b2, da + db
    p3, q3 = e1 - b2, db - da
    return [u0 + u1, p1 + q1, w0 + w1, p3 + q3, u0 - u1, p1 - q1, w0 - w1, p3 - q3]


def sigmoid(v):
    return 0.5 + 0.5 * jnp.tanh(0.5 * v)


def split(v):
    high = v.astype(BF16)
    return high, (v - high.astype(F32)).astype(BF16)


def iota(shape, dim):
    return lax.broadcasted_iota(jnp.int32, shape, dim)


def kernel(
    n,
    slots,
    rows_own,
    slide_ref,
    mask_ref,
    label_ref,
    tiles_ref,
    field_ref,
    lift_ref,
    group_ref,
    class_ref,
    margins_ref,
    out_ref,
    raw_w,
    wts,
    feat,
    prod,
    slope,
    lift_a,
    base,
    lgrad,
    fbuf,
    isrc,
    ibuf,
    gsrc,
    gbuf,
    wsem,
    fsend,
    frecv,
    isend,
    irecv,
    gsend,
    grecv,
):
    me = lax.axis_index("tiles")
    slides_own = 2 * rows_own
    pixels = slots * PIX
    row = 8 * slots
    classes = class_ref.shape[1]

    for tap in range(9):
        pltpu.make_async_copy(group_ref.at[:, tap], raw_w.at[tap], wsem.at[tap]).start()

    barrier = pltpu.get_barrier_semaphore()

    def greet(step, carry):
        pl.semaphore_signal(barrier, inc=1, device_id={"tiles": lax.rem(me + step, n)})
        return carry

    lax.fori_loop(1, n, greet, 0)

    sub8 = iota((8, LANES), 0)
    ids = jnp.full((8, LANES), -1.0, F32)
    for slot in range(slots):
        code = jnp.where(mask_ref[slot] > 0, slide_ref[slot], -1).astype(F32)
        ids = jnp.where(sub8 == slot, code, ids)
    isrc[...] = ids
    ibuf[me] = ids
    fbuf[me] = field_ref[...]
    pl.semaphore_wait(barrier, n - 1)

    def send_first(step, carry):
        peer = {"tiles": lax.rem(me + step, n)}
        pltpu.make_async_remote_copy(
            field_ref, fbuf.at[me], fsend, frecv, device_id=peer
        ).start()
        pltpu.make_async_remote_copy(isrc, ibuf.at[me], isend, irecv, device_id=peer).start()
        return carry

    lax.fori_loop(1, n, send_first, 0)

    zeros_pad = jnp.zeros((row, 256), BF16)
    for freq in range(4):
        for shift in range(3):
            feat[freq, shift, 0:row, :] = zeros_pad
            feat[freq, shift, pixels + row : pixels + 2 * row, :] = zeros_pad

    lift_a[...] = jnp.zeros_like(lift_a)
    for tap in range(9):
        part = lift_ref[tap]
        l0, l1, l2 = part[0:1], part[1:2], part[2:3]
        mean = (l0 + l1 + l2) * (1.0 / 3.0)
        crossed = (CROSS * (l1 - l2), CROSS * (l2 - l0), CROSS * (l0 - l1))
        for colour, own in enumerate((l0, l1, l2)):
            at = slice(tap * 8 + colour, tap * 8 + colour + 1)
            lift_a[at, 0:128] = mean
            lift_a[at, 128:256] = own - mean
            lift_a[at, 256:384] = crossed[colour]
    lift_high, lift_low = split(lift_a[...])

    def prepare(tap, carry):
        pltpu.make_async_copy(group_ref.at[:, tap], raw_w.at[tap], wsem.at[tap]).wait()
        for start in range(0, 128, 32):
            x = [raw_w[tap, hue, start : start + 32, :].astype(F32) for hue in range(8)]
            parts = hue_transform(x)
            top, bottom = slice(start, start + 32), slice(128 + start, 160 + start)
            nothing = jnp.zeros((32, 128), BF16)
            wts[0, tap, top, 0:128] = (parts[0][0] * 0.125).astype(BF16)
            wts[0, tap, top, 128:256] = nothing
            wts[0, tap, bottom, 0:128] = nothing
            wts[0, tap, bottom, 128:256] = (parts[0][1] * 0.125).astype(BF16)
            for freq in range(1, 4):
                p = (parts[freq][0] * 0.25).astype(BF16)
                q = (parts[freq][1] * 0.25).astype(BF16)
                wts[freq, tap, top, 0:128] = p
                wts[freq, tap, top, 128:256] = -q
                wts[freq, tap, bottom, 0:128] = q
                wts[freq, tap, bottom, 128:256] = p
        return carry

    lax.fori_loop(0, 9, prepare, 0)

    row_slot = iota((row, classes), 0) // 8
    label_col = jnp.full((row, classes), -1, jnp.int32)
    live_col = jnp.zeros((row, classes), F32)
    for slot in range(slots):
        label_col = jnp.where(row_slot == slot, label_ref[slot], label_col)
        live_col = jnp.where(row_slot == slot, mask_ref[slot].astype(F32), live_col)
    hot = (label_col == iota((row, classes), 1)).astype(F32)
    score_grad = PIX * live_col * (1.0 / classes - hot)
    spread = lax.dot_general(
        score_grad,
        class_ref[...],
        (((1,), (1,)), ((), ())),
        precision=HIGHEST,
        preferred_element_type=F32,
    ) * (1.0 / 512.0)

    src = iota((pixels, pixels), 0)
    dst = iota((pixels, pixels), 1)
    moved = (dst // 8) % slots * PIX + dst // row * 8 + dst % 8
    permute = (src == moved).astype(F32)

    pltpu.make_async_copy(fbuf.at[pl.ds(0, n - 1)], fbuf.at[pl.ds(0, n - 1)], frecv).wait()
    lane = iota((1, LANES), 1)
    halves = []
    for slot in range(slots):
        slide = slide_ref[slot]
        owner = slide // slides_own
        local = slide - owner * slides_own
        own_row = local // 2
        odd = (local - 2 * own_row).astype(F32)
        found = fbuf[owner, pl.ds(own_row, 1), :]
        turned = pltpu.roll(found, 64, 1)
        if slot % 2:
            odd = 1.0 - odd
        halves.append(found * (1.0 - odd) + turned * odd)
    angle_row = jnp.concatenate(
        [jnp.where(lane < 64, halves[i], halves[i + 1]) for i in range(0, slots, 2)], axis=1
    )
    sub = iota((8, pixels), 0)
    colours = tiles_ref[...].astype(F32)
    inputs = jnp.where(sub == 3, angle_row, 0.0)
    for colour in range(3):
        inputs = jnp.where(sub == colour, colours[colour : colour + 1], inputs)
    inputs = jnp.dot(inputs, permute, precision=HIGHEST, preferred_element_type=F32)
    red, green, blue = inputs[0:1], inputs[1:2], inputs[2:3]
    cos_angle, sin_angle = jnp.cos(inputs[3:4]), jnp.sin(inputs[3:4])
    grey = (red + green + blue) * (1.0 / 3.0)

    def stack3(rows):
        result = jnp.where(sub == 0, rows[0], 0.0)
        result = jnp.where(sub == 1, rows[1], result)
        return jnp.where(sub == 2, rows[2], result)

    crosses = (CROSS * (blue - green), CROSS * (red - blue), CROSS * (green - red))
    attacked = stack3(
        [
            cos_angle * x + sin_angle * y + (1.0 - cos_angle) * grey
            for x, y in zip((red, green, blue), crosses)
        ]
    )
    turning = stack3(
        [
            -sin_angle * x + cos_angle * y + sin_angle * grey
            for x, y in zip((red, green, blue), crosses)
        ]
    )
    lanes = iota((8, pixels), 1)
    lane_y, lane_x = lanes // row, lanes % 8

    def moved_by(value, dy, dx):
        distance = dy * row + dx
        if distance:
            value = pltpu.roll(value, (-distance) % pixels, 1)
        inside = (lane_y + dy >= 0) & (lane_y + dy < 8) & (lane_x + dx >= 0) & (lane_x + dx < 8)
        return jnp.where(inside, value, 0.0)

    patches = jnp.concatenate(
        [moved_by(attacked, dy, dx) for dy, dx in TAPS] + [jnp.zeros((8, pixels), F32)], axis=0
    )
    patch_high, patch_low = split(patches)
    base[...] = lax.dot_general(
        jnp.concatenate([patch_high, patch_low, patch_high], axis=0),
        jnp.concatenate([lift_high, lift_high, lift_low], axis=0),
        (((0,), (0,)), ((), ())),
        preferred_element_type=F32,
    )

    first = iota((slots, 8, 128), 1) == 0
    last = iota((slots, 8, 128), 1) == 7

    def put(y, values):
        at = pl.ds(pl.multiple_of(row + y * row, row), row)
        for freq, pair in enumerate(hue_transform(values)):
            for side, value in enumerate(pair):
                cols = slice(128 * side, 128 * side + 128)
                block = value.reshape(slots, 8, 128)
                left = jnp.where(first, 0.0, pltpu.roll(block, 1, 1)).reshape(row, 128)
                right = jnp.where(last, 0.0, pltpu.roll(block, 7, 1)).reshape(row, 128)
                feat[freq, 0, at, cols] = left.astype(BF16)
                feat[freq, 1, at, cols] = value.astype(BF16)
                feat[freq, 2, at, cols] = right.astype(BF16)

    def convolve(forward):
        def one(freq, carry):
            total = jnp.zeros((pixels, 256), F32)
            for tap, (dy, dx) in enumerate(TAPS):
                if not forward:
                    dy, dx = -dy, -dx
                start = (dy + 1) * row
                total = total + lax.dot_general(
                    feat[freq, dx + 1, start : start + pixels, :],
                    wts[freq, tap],
                    (((1,), (0 if forward else 1,)), ((), ())),
                    preferred_element_type=F32,
                )
            prod[freq] = total
            return carry

        lax.fori_loop(0, 4, one, 0)

    def take(at):
        return hue_spread([(prod[f, at, 0:128], prod[f, at, 128:256]) for f in range(4)])

    def activate(y, carry):
        at = pl.ds(pl.multiple_of(y * row, row), row)
        b0, bc, bs = base[at, 0:128], base[at, 128:256], base[at, 256:384]
        d1 = ROOT_HALF * (bc - bs)
        d3 = ROOT_HALF * (bc + bs)
        lifted = [b0 + bc, b0 + d1, b0 - bs, b0 - d3, b0 - bc, b0 - d1, b0 + bs, b0 + d3]
        acts = []
        for hue, v in enumerate(lifted):
            g = sigmoid(v)
            act = v * g
            slope[hue, at, :] = g + act * (1.0 - g)
            acts.append(act)
        put(y, acts)
        return carry

    lax.fori_loop(0, 8, activate, 0)
    convolve(True)

    def middle(y, pooled):
        at = pl.ds(pl.multiple_of(y * row, row), row)
        grads = []
        for v in take(at):
            g = sigmoid(v)
            act = v * g
            pooled = pooled + act
            grads.append(spread * (g + act * (1.0 - g)))
        put(y, grads)
        return pooled

    pooled = lax.fori_loop(0, 8, middle, jnp.zeros((row, 128), F32))
    convolve(False)

    def finish(y, carry):
        at = pl.ds(pl.multiple_of(y * row, row), row)
        grads = [grad * slope[hue, at, :] for hue, grad in enumerate(take(at))]
        parts = hue_transform(grads)
        for place, value in enumerate((parts[0][0], parts[1][0], -parts[1][1])):
            cols = slice(128 * place, 128 * place + 128)
            high, low = split(value)
            lgrad[0, at, cols] = high
            lgrad[1, at, cols] = low
        return carry

    lax.fori_loop(0, 8, finish, 0)

    nt = (((1,), (1,)), ((), ()))
    both = lax.dot_general(
        jnp.concatenate([lift_high, lift_low], axis=0), lgrad[0], nt, preferred_element_type=F32
    )
    patch_grad = (
        both[0:80] + both[80:160]
        + lax.dot_general(lift_high, lgrad[1], nt, preferred_element_type=F32)
    )
    colour_grad = jnp.zeros((8, pixels), F32)
    for tap, (dy, dx) in enumerate(TAPS):
        colour_grad = colour_grad + moved_by(patch_grad[tap * 8 : tap * 8 + 8], -dy, -dx)
    angle_grad = jnp.sum(colour_grad * turning, axis=0, keepdims=True)
    by_slot = jnp.where((lanes // 8) % slots == sub, angle_grad, 0.0)
    pick_src = iota((pixels, 128), 0)
    pick = (pick_src // row * 8 + pick_src % 8 == iota((pixels, 128), 1)).astype(F32)
    grads = jnp.dot(by_slot, pick, precision=HIGHEST, preferred_element_type=F32)
    gsrc[...] = grads
    gbuf[me] = grads

    def send_second(step, carry):
        peer = {"tiles": lax.rem(me + step, n)}
        pltpu.make_async_remote_copy(gsrc, gbuf.at[me], gsend, grecv, device_id=peer).start()
        return carry

    lax.fori_loop(1, n, send_second, 0)

    scored = pooled * spread
    for slot in range(slots):
        margins_ref[slot] = -jnp.sum(scored[8 * slot : 8 * slot + 8]) * (1.0 / PIX)

    others = pl.ds(0, n - 1)
    pltpu.make_async_copy(ibuf.at[others], ibuf.at[others], irecv).wait()
    codes = ibuf[...].reshape(n * 8, LANES)
    col = iota((n * 8, LANES), 1)
    wanted = jnp.where(col < 64, 2 * col, 2 * (col - 64) + 1)
    wanted = jnp.where(col % 64 < rows_own, wanted + me * slides_own, -2)
    chooser = (codes == wanted.astype(F32)).astype(BF16)

    pltpu.make_async_copy(gbuf.at[others], gbuf.at[others], grecv).wait()
    gathered = gbuf[...].reshape(n * 8, LANES)
    gathered = jnp.where(col < 64, gathered, 1.0)
    high, low = split(gathered)
    tn = (((0,), (0,)), ((), ()))
    sums = lax.dot_general(chooser, high, tn, preferred_element_type=F32) + lax.dot_general(
        chooser, low, tn, preferred_element_type=F32
    )

    def averaged(block):
        return block / jnp.maximum(pltpu.roll(block, 64, 1), 1.0)

    even, odd = averaged(sums[0:64]), averaged(sums[64:128])
    left = iota((64, LANES), 1) < 64
    out_ref[...] = jnp.where(left, even, pltpu.roll(odd, 64, 1))[0:rows_own]

    pltpu.make_async_copy(fbuf.at[others], fbuf.at[others], fsend).wait()
    pltpu.make_async_copy(ibuf.at[others], ibuf.at[others], isend).wait()
    pltpu.make_async_copy(gbuf.at[others], gbuf.at[others], gsend).wait()


def solution(mesh):
    n = mesh.shape["tiles"]

    def shards(tiles, slide, mask, label, field, lift_weight, group_weight, class_weight):
        slots = slide.shape[0]
        rows_own = field.shape[0] // LANES
        pixels = slots * PIX
        vmem = pl.BlockSpec(memory_space=pltpu.VMEM)
        smem = pl.BlockSpec(memory_space=pltpu.SMEM)
        margins, grads = pl.pallas_call(
            functools.partial(kernel, n, slots, rows_own),
            out_shape=(
                jax.ShapeDtypeStruct((slots,), F32),
                jax.ShapeDtypeStruct((rows_own, LANES), F32),
            ),
            in_specs=[smem, smem, smem, vmem, vmem, vmem, pl.BlockSpec(memory_space=pl.ANY), vmem],
            out_specs=(smem, vmem),
            scratch_shapes=[
                pltpu.VMEM((9, 8, 128, 128), BF16),
                pltpu.VMEM((4, 9, 256, 256), BF16),
                pltpu.VMEM((4, 3, pixels + 16 * slots, 256), BF16),
                pltpu.VMEM((4, pixels, 256), F32),
                pltpu.VMEM((8, pixels, 128), F32),
                pltpu.VMEM((80, 384), F32),
                pltpu.VMEM((pixels, 384), F32),
                pltpu.VMEM((2, pixels, 384), BF16),
                pltpu.VMEM((n, rows_own, LANES), F32),
                pltpu.VMEM((8, LANES), F32),
                pltpu.VMEM((n, 8, LANES), F32),
                pltpu.VMEM((8, LANES), F32),
                pltpu.VMEM((n, 8, LANES), F32),
                pltpu.SemaphoreType.DMA((9,)),
            ]
            + [pltpu.SemaphoreType.DMA] * 6,
            compiler_params=pltpu.CompilerParams(
                collective_id=0, has_side_effects=True, vmem_limit_bytes=48 << 20
            ),
        )(
            slide,
            mask,
            label,
            tiles,
            field.reshape(rows_own, LANES),
            lift_weight,
            group_weight,
            class_weight,
        )
        return margins, grads.reshape(-1)

    split_all = P(("groups", "tiles"))
    return jax.shard_map(
        shards,
        mesh=mesh,
        in_specs=(
            P(None, ("groups", "tiles")),
            split_all,
            split_all,
            split_all,
            split_all,
            P(),
            P(),
            P(),
        ),
        out_specs=(split_all, split_all),
        check_vma=False,
    )
```

```python
import functools
import math

import jax
import jax.numpy as jnp
from jax import lax
from jax.experimental import pallas as pl
from jax.experimental.pallas import tpu as pltpu
from jax.sharding import PartitionSpec as P

F32 = jnp.float32
BF16 = jnp.bfloat16
HIGHEST = lax.Precision.HIGHEST
ROOT_HALF = math.sqrt(0.5)
CROSS = 1.0 / math.sqrt(3.0)
PIX = 64
LANES = 128
TAPS = [(tap // 3 - 1, tap % 3 - 1) for tap in range(9)]


def hue_transform(x):
    s04, d04 = x[0] + x[4], x[0] - x[4]
    s15, d15 = x[1] + x[5], x[1] - x[5]
    s26, d26 = x[2] + x[6], x[2] - x[6]
    s37, d37 = x[3] + x[7], x[3] - x[7]
    even, odd = s04 + s26, s15 + s37
    dc = ROOT_HALF * (d15 - d37)
    ds = ROOT_HALF * (d15 + d37)
    return [
        (even + odd, even - odd),
        (d04 + dc, d26 + ds),
        (s04 - s26, s15 - s37),
        (d04 - dc, ds - d26),
    ]


def hue_spread(parts):
    (c0, c4), (a1, b1), (a2, b2), (a3, b3) = parts
    e0, e1 = c0 + c4, c0 - c4
    u0, u1 = e0 + a2, a1 + a3
    w0, w1 = e0 - a2, b1 - b3
    da = ROOT_HALF * (a1 - a3)
    db = ROOT_HALF * (b1 + b3)
    p1, q1 = e1 + b2, da + db
    p3, q3 = e1 - b2, db - da
    return [u0 + u1, p1 + q1, w0 + w1, p3 + q3, u0 - u1, p1 - q1, w0 - w1, p3 - q3]


def sigmoid(v):
    return 0.5 + 0.5 * jnp.tanh(0.5 * v)


def split(v):
    high = v.astype(BF16)
    return high, (v - high.astype(F32)).astype(BF16)


def iota(shape, dim):
    return lax.broadcasted_iota(jnp.int32, shape, dim)


def kernel(
    n,
    slots,
    rows_own,
    slide_in,
    mask_in,
    label_in,
    tiles_in,
    field_ref,
    lift_in,
    group_ref,
    class_in,
    margins_ref,
    out_ref,
    slide_ref,
    mask_ref,
    label_ref,
    tiles_ref,
    lift_ref,
    class_ref,
    raw_w,
    wts,
    feat,
    prod,
    slope,
    lift_a,
    base,
    lgrad,
    fbuf,
    isrc,
    ibuf,
    gsrc,
    gbuf,
    insem,
    wsem,
    fsend,
    frecv,
    isend,
    irecv,
    gsend,
    grecv,
):
    me = lax.axis_index("tiles")
    slides_own = 2 * rows_own
    pixels = slots * PIX
    row = 8 * slots
    classes = class_ref.shape[0]

    loads = [
        pltpu.make_async_copy(source, target, insem.at[place])
        for place, (source, target) in enumerate(
            (
                (slide_in, slide_ref),
                (mask_in, mask_ref),
                (label_in, label_ref),
                (tiles_in, tiles_ref),
                (lift_in, lift_ref),
                (class_in, class_ref),
                (field_ref, fbuf.at[me]),
            )
        )
    ]
    for load in loads:
        load.start()
    for tap in range(9):
        pltpu.make_async_copy(group_ref.at[:, tap], raw_w.at[tap], wsem.at[tap]).start()

    barrier = pltpu.get_barrier_semaphore()

    def greet(step, carry):
        pl.semaphore_signal(barrier, inc=1, device_id={"tiles": lax.rem(me + step, n)})
        return carry

    lax.fori_loop(1, n, greet, 0)

    for load in loads:
        load.wait()
    sub8 = iota((8, LANES), 0)
    ids = jnp.full((8, LANES), -1.0, F32)
    for slot in range(slots):
        code = jnp.where(mask_ref[slot] > 0, slide_ref[slot], -1).astype(F32)
        ids = jnp.where(sub8 == slot, code, ids)
    isrc[...] = ids
    ibuf[me] = ids
    pl.semaphore_wait(barrier, n - 1)

    def send_first(step, carry):
        peer = {"tiles": lax.rem(me + step, n)}
        pltpu.make_async_remote_copy(
            field_ref, fbuf.at[me], fsend, frecv, device_id=peer
        ).start()
        pltpu.make_async_remote_copy(isrc, ibuf.at[me], isend, irecv, device_id=peer).start()
        return carry

    lax.fori_loop(1, n, send_first, 0)

    zeros_pad = jnp.zeros((row, 256), BF16)
    for freq in range(4):
        for shift in range(3):
            feat[freq, shift, 0:row, :] = zeros_pad
            feat[freq, shift, pixels + row : pixels + 2 * row, :] = zeros_pad

    lift_a[...] = jnp.zeros_like(lift_a)
    for tap in range(9):
        part = lift_ref[tap]
        l0, l1, l2 = part[0:1], part[1:2], part[2:3]
        mean = (l0 + l1 + l2) * (1.0 / 3.0)
        crossed = (CROSS * (l1 - l2), CROSS * (l2 - l0), CROSS * (l0 - l1))
        for colour, own in enumerate((l0, l1, l2)):
            at = slice(tap * 8 + colour, tap * 8 + colour + 1)
            lift_a[at, 0:128] = mean
            lift_a[at, 128:256] = own - mean
            lift_a[at, 256:384] = crossed[colour]
    lift_high, lift_low = split(lift_a[...])

    def prepare(tap, carry):
        pltpu.make_async_copy(group_ref.at[:, tap], raw_w.at[tap], wsem.at[tap]).wait()
        for start in range(0, 128, 32):
            x = [raw_w[tap, hue, start : start + 32, :].astype(F32) for hue in range(8)]
            parts = hue_transform(x)
            top, bottom = slice(start, start + 32), slice(128 + start, 160 + start)
            nothing = jnp.zeros((32, 128), BF16)
            wts[0, tap, top, 0:128] = (parts[0][0] * 0.125).astype(BF16)
            wts[0, tap, top, 128:256] = nothing
            wts[0, tap, bottom, 0:128] = nothing
            wts[0, tap, bottom, 128:256] = (parts[0][1] * 0.125).astype(BF16)
            for freq in range(1, 4):
                p = (parts[freq][0] * 0.25).astype(BF16)
                q = (parts[freq][1] * 0.25).astype(BF16)
                wts[freq, tap, top, 0:128] = p
                wts[freq, tap, top, 128:256] = -q
                wts[freq, tap, bottom, 0:128] = q
                wts[freq, tap, bottom, 128:256] = p
        return carry

    lax.fori_loop(0, 9, prepare, 0)

    row_slot = iota((row, classes), 0) // 8
    label_col = jnp.full((row, classes), -1, jnp.int32)
    live_col = jnp.zeros((row, classes), F32)
    for slot in range(slots):
        label_col = jnp.where(row_slot == slot, label_ref[slot], label_col)
        live_col = jnp.where(row_slot == slot, mask_ref[slot].astype(F32), live_col)
    hot = (label_col == iota((row, classes), 1)).astype(F32)
    score_grad = PIX * live_col * (1.0 / classes - hot)
    spread = lax.dot_general(
        score_grad,
        class_ref[...],
        (((1,), (0,)), ((), ())),
        precision=HIGHEST,
        preferred_element_type=F32,
    ) * (1.0 / 512.0)

    src = iota((pixels, pixels), 0)
    dst = iota((pixels, pixels), 1)
    moved = (dst // 8) % slots * PIX + dst // row * 8 + dst % 8
    permute = (src == moved).astype(F32)

    pltpu.make_async_copy(fbuf.at[pl.ds(0, n - 1)], fbuf.at[pl.ds(0, n - 1)], frecv).wait()
    lane = iota((1, LANES), 1)
    halves = []
    for slot in range(slots):
        slide = slide_ref[slot]
        owner = slide // slides_own
        local = slide - owner * slides_own
        own_row = local // 2
        odd = (local - 2 * own_row).astype(F32)
        found = fbuf[owner, pl.ds(own_row, 1), :]
        turned = pltpu.roll(found, 64, 1)
        if slot % 2:
            odd = 1.0 - odd
        halves.append(found * (1.0 - odd) + turned * odd)
    angle_row = jnp.concatenate(
        [jnp.where(lane < 64, halves[i], halves[i + 1]) for i in range(0, slots, 2)], axis=1
    )
    sub = iota((8, pixels), 0)
    colours = tiles_ref[...].astype(F32)
    inputs = jnp.where(sub == 3, angle_row, 0.0)
    for colour in range(3):
        inputs = jnp.where(sub == colour, colours[colour : colour + 1], inputs)
    inputs = jnp.dot(inputs, permute, precision=HIGHEST, preferred_element_type=F32)
    red, green, blue = inputs[0:1], inputs[1:2], inputs[2:3]
    cos_angle, sin_angle = jnp.cos(inputs[3:4]), jnp.sin(inputs[3:4])
    grey = (red + green + blue) * (1.0 / 3.0)

    def stack3(rows):
        result = jnp.where(sub == 0, rows[0], 0.0)
        result = jnp.where(sub == 1, rows[1], result)
        return jnp.where(sub == 2, rows[2], result)

    crosses = (CROSS * (blue - green), CROSS * (red - blue), CROSS * (green - red))
    attacked = stack3(
        [
            cos_angle * x + sin_angle * y + (1.0 - cos_angle) * grey
            for x, y in zip((red, green, blue), crosses)
        ]
    )
    turning = stack3(
        [
            -sin_angle * x + cos_angle * y + sin_angle * grey
            for x, y in zip((red, green, blue), crosses)
        ]
    )
    lanes = iota((8, pixels), 1)
    lane_y, lane_x = lanes // row, lanes % 8

    def moved_by(value, dy, dx):
        distance = dy * row + dx
        if distance:
            value = pltpu.roll(value, (-distance) % pixels, 1)
        inside = (lane_y + dy >= 0) & (lane_y + dy < 8) & (lane_x + dx >= 0) & (lane_x + dx < 8)
        return jnp.where(inside, value, 0.0)

    patches = jnp.concatenate(
        [moved_by(attacked, dy, dx) for dy, dx in TAPS] + [jnp.zeros((8, pixels), F32)], axis=0
    )
    patch_high, patch_low = split(patches)
    base[...] = lax.dot_general(
        jnp.concatenate([patch_high, patch_low, patch_high], axis=0),
        jnp.concatenate([lift_high, lift_high, lift_low], axis=0),
        (((0,), (0,)), ((), ())),
        preferred_element_type=F32,
    )

    first = iota((slots, 8, 128), 1) == 0
    last = iota((slots, 8, 128), 1) == 7

    def put(y, values):
        at = pl.ds(pl.multiple_of(row + y * row, row), row)
        for freq, pair in enumerate(hue_transform(values)):
            for side, value in enumerate(pair):
                cols = slice(128 * side, 128 * side + 128)
                block = value.reshape(slots, 8, 128)
                left = jnp.where(first, 0.0, pltpu.roll(block, 1, 1)).reshape(row, 128)
                right = jnp.where(last, 0.0, pltpu.roll(block, 7, 1)).reshape(row, 128)
                feat[freq, 0, at, cols] = left.astype(BF16)
                feat[freq, 1, at, cols] = value.astype(BF16)
                feat[freq, 2, at, cols] = right.astype(BF16)

    def convolve(forward):
        def one(freq, carry):
            total = jnp.zeros((pixels, 256), F32)
            for tap, (dy, dx) in enumerate(TAPS):
                if not forward:
                    dy, dx = -dy, -dx
                start = (dy + 1) * row
                total = total + lax.dot_general(
                    feat[freq, dx + 1, start : start + pixels, :],
                    wts[freq, tap],
                    (((1,), (0 if forward else 1,)), ((), ())),
                    preferred_element_type=F32,
                )
            prod[freq] = total
            return carry

        lax.fori_loop(0, 4, one, 0)

    def take(at):
        return hue_spread([(prod[f, at, 0:128], prod[f, at, 128:256]) for f in range(4)])

    def activate(y, carry):
        at = pl.ds(pl.multiple_of(y * row, row), row)
        b0, bc, bs = base[at, 0:128], base[at, 128:256], base[at, 256:384]
        d1 = ROOT_HALF * (bc - bs)
        d3 = ROOT_HALF * (bc + bs)
        lifted = [b0 + bc, b0 + d1, b0 - bs, b0 - d3, b0 - bc, b0 - d1, b0 + bs, b0 + d3]
        acts = []
        for hue, v in enumerate(lifted):
            g = sigmoid(v)
            act = v * g
            slope[hue, at, :] = g + act * (1.0 - g)
            acts.append(act)
        put(y, acts)
        return carry

    lax.fori_loop(0, 8, activate, 0)
    convolve(True)

    def middle(y, pooled):
        at = pl.ds(pl.multiple_of(y * row, row), row)
        grads = []
        for v in take(at):
            g = sigmoid(v)
            act = v * g
            pooled = pooled + act
            grads.append(spread * (g + act * (1.0 - g)))
        put(y, grads)
        return pooled

    pooled = lax.fori_loop(0, 8, middle, jnp.zeros((row, 128), F32))
    convolve(False)

    def finish(y, carry):
        at = pl.ds(pl.multiple_of(y * row, row), row)
        grads = [grad * slope[hue, at, :] for hue, grad in enumerate(take(at))]
        parts = hue_transform(grads)
        for place, value in enumerate((parts[0][0], parts[1][0], -parts[1][1])):
            cols = slice(128 * place, 128 * place + 128)
            high, low = split(value)
            lgrad[0, at, cols] = high
            lgrad[1, at, cols] = low
        return carry

    lax.fori_loop(0, 8, finish, 0)

    nt = (((1,), (1,)), ((), ()))
    both = lax.dot_general(
        jnp.concatenate([lift_high, lift_low], axis=0), lgrad[0], nt, preferred_element_type=F32
    )
    patch_grad = (
        both[0:80] + both[80:160]
        + lax.dot_general(lift_high, lgrad[1], nt, preferred_element_type=F32)
    )
    colour_grad = jnp.zeros((8, pixels), F32)
    for tap, (dy, dx) in enumerate(TAPS):
        colour_grad = colour_grad + moved_by(patch_grad[tap * 8 : tap * 8 + 8], -dy, -dx)
    angle_grad = jnp.sum(colour_grad * turning, axis=0, keepdims=True)
    by_slot = jnp.where((lanes // 8) % slots == sub, angle_grad, 0.0)
    pick_src = iota((pixels, 128), 0)
    pick = (pick_src // row * 8 + pick_src % 8 == iota((pixels, 128), 1)).astype(F32)
    grads = jnp.dot(by_slot, pick, precision=HIGHEST, preferred_element_type=F32)
    gsrc[...] = grads
    gbuf[me] = grads

    def send_second(step, carry):
        peer = {"tiles": lax.rem(me + step, n)}
        pltpu.make_async_remote_copy(gsrc, gbuf.at[me], gsend, grecv, device_id=peer).start()
        return carry

    lax.fori_loop(1, n, send_second, 0)

    scored = pooled * spread
    for slot in range(slots):
        margins_ref[slot] = -jnp.sum(scored[8 * slot : 8 * slot + 8]) * (1.0 / PIX)

    others = pl.ds(0, n - 1)
    pltpu.make_async_copy(ibuf.at[others], ibuf.at[others], irecv).wait()
    codes = ibuf[...].reshape(n * 8, LANES)
    col = iota((n * 8, LANES), 1)
    wanted = jnp.where(col < 64, 2 * col, 2 * (col - 64) + 1)
    wanted = jnp.where(col % 64 < rows_own, wanted + me * slides_own, -2)
    chooser = (codes == wanted.astype(F32)).astype(BF16)

    pltpu.make_async_copy(gbuf.at[others], gbuf.at[others], grecv).wait()
    gathered = gbuf[...].reshape(n * 8, LANES)
    gathered = jnp.where(col < 64, gathered, 1.0)
    high, low = split(gathered)
    tn = (((0,), (0,)), ((), ()))
    sums = lax.dot_general(chooser, high, tn, preferred_element_type=F32) + lax.dot_general(
        chooser, low, tn, preferred_element_type=F32
    )

    def averaged(block):
        return block / jnp.maximum(pltpu.roll(block, 64, 1), 1.0)

    even, odd = averaged(sums[0:64]), averaged(sums[64:128])
    left = iota((64, LANES), 1) < 64
    out_ref[...] = jnp.where(left, even, pltpu.roll(odd, 64, 1))[0:rows_own]

    pltpu.make_async_copy(fbuf.at[others], fbuf.at[others], fsend).wait()
    pltpu.make_async_copy(ibuf.at[others], ibuf.at[others], isend).wait()
    pltpu.make_async_copy(gbuf.at[others], gbuf.at[others], gsend).wait()


def solution(mesh):
    n = mesh.shape["tiles"]

    def shards(tiles, slide, mask, label, field, lift_weight, group_weight, class_weight):
        slots = slide.shape[0]
        rows_own = field.shape[0] // LANES
        pixels = slots * PIX
        vmem = pl.BlockSpec(memory_space=pltpu.VMEM)
        smem = pl.BlockSpec(memory_space=pltpu.SMEM)
        margins, grads = pl.pallas_call(
            functools.partial(kernel, n, slots, rows_own),
            out_shape=(
                jax.ShapeDtypeStruct((slots,), F32),
                jax.ShapeDtypeStruct((rows_own, LANES), F32),
            ),
            in_specs=[pl.BlockSpec(memory_space=pltpu.HBM)] * 8,
            out_specs=(smem, vmem),
            scratch_shapes=[
                pltpu.SMEM((slots,), jnp.int32),
                pltpu.SMEM((slots,), jnp.int32),
                pltpu.SMEM((slots,), jnp.int32),
                pltpu.VMEM((3, pixels), BF16),
                pltpu.VMEM(lift_weight.shape, F32),
                pltpu.VMEM(class_weight.shape[::-1], F32),
                pltpu.VMEM((9, 8, 128, 128), BF16),
                pltpu.VMEM((4, 9, 256, 256), BF16),
                pltpu.VMEM((4, 3, pixels + 16 * slots, 256), BF16),
                pltpu.VMEM((4, pixels, 256), F32),
                pltpu.VMEM((8, pixels, 128), F32),
                pltpu.VMEM((80, 384), F32),
                pltpu.VMEM((pixels, 384), F32),
                pltpu.VMEM((2, pixels, 384), BF16),
                pltpu.VMEM((n, rows_own, LANES), F32),
                pltpu.VMEM((8, LANES), F32),
                pltpu.VMEM((n, 8, LANES), F32),
                pltpu.VMEM((8, LANES), F32),
                pltpu.VMEM((n, 8, LANES), F32),
                pltpu.SemaphoreType.DMA((7,)),
                pltpu.SemaphoreType.DMA((9,)),
            ]
            + [pltpu.SemaphoreType.DMA] * 6,
            compiler_params=pltpu.CompilerParams(
                collective_id=0, has_side_effects=True, vmem_limit_bytes=67_000_000
            ),
        )(
            slide,
            mask,
            label,
            tiles,
            field.reshape(rows_own, LANES),
            lift_weight,
            group_weight,
            class_weight.T,
        )
        return margins, grads.reshape(-1)

    split_all = P(("groups", "tiles"))
    return jax.shard_map(
        shards,
        mesh=mesh,
        in_specs=(
            P(None, ("groups", "tiles")),
            split_all,
            split_all,
            split_all,
            split_all,
            P(),
            P(),
            P(),
        ),
        out_specs=(split_all, split_all),
        check_vma=False,
    )
```

```python
import functools
import math

import jax
import jax.numpy as jnp
from jax import lax
from jax.experimental import pallas as pl
from jax.experimental.pallas import tpu as pltpu
from jax.sharding import PartitionSpec as P

F32 = jnp.float32
BF16 = jnp.bfloat16
HIGHEST = lax.Precision.HIGHEST
ROOT_HALF = math.sqrt(0.5)
CROSS = 1.0 / math.sqrt(3.0)
PIX = 64
LANES = 128
TAPS = [(tap // 3 - 1, tap % 3 - 1) for tap in range(9)]


def hue_transform(x):
    s04, d04 = x[0] + x[4], x[0] - x[4]
    s15, d15 = x[1] + x[5], x[1] - x[5]
    s26, d26 = x[2] + x[6], x[2] - x[6]
    s37, d37 = x[3] + x[7], x[3] - x[7]
    even, odd = s04 + s26, s15 + s37
    dc = ROOT_HALF * (d15 - d37)
    ds = ROOT_HALF * (d15 + d37)
    return [
        (even + odd, even - odd),
        (d04 + dc, d26 + ds),
        (s04 - s26, s15 - s37),
        (d04 - dc, ds - d26),
    ]


def hue_spread(parts):
    (c0, c4), (a1, b1), (a2, b2), (a3, b3) = parts
    e0, e1 = c0 + c4, c0 - c4
    u0, u1 = e0 + a2, a1 + a3
    w0, w1 = e0 - a2, b1 - b3
    da = ROOT_HALF * (a1 - a3)
    db = ROOT_HALF * (b1 + b3)
    p1, q1 = e1 + b2, da + db
    p3, q3 = e1 - b2, db - da
    return [u0 + u1, p1 + q1, w0 + w1, p3 + q3, u0 - u1, p1 - q1, w0 - w1, p3 - q3]


def sigmoid(v):
    return 0.5 + 0.5 * jnp.tanh(0.5 * v)


def split(v):
    high = v.astype(BF16)
    return high, (v - high.astype(F32)).astype(BF16)


def iota(shape, dim):
    return lax.broadcasted_iota(jnp.int32, shape, dim)


def kernel(
    n,
    slots,
    rows_own,
    slide_in,
    mask_in,
    label_in,
    tiles_in,
    field_ref,
    lift_in,
    group_ref,
    class_in,
    margins_ref,
    out_ref,
    slide_ref,
    mask_ref,
    label_ref,
    tiles_ref,
    lift_ref,
    class_ref,
    raw_w,
    wts,
    feat,
    prod,
    slope,
    lift_a,
    base,
    lgrad,
    fbuf,
    isrc,
    ibuf,
    gsrc,
    gbuf,
    insem,
    wsem,
    fsend,
    frecv,
    isend,
    irecv,
    gsend,
    grecv,
):
    me = lax.axis_index("tiles")
    slides_own = 2 * rows_own
    pixels = slots * PIX
    row = 8 * slots
    pairs = slots // 2
    classes = class_ref.shape[0]

    gbuf[...] = jnp.zeros_like(gbuf)
    barrier = pltpu.get_barrier_semaphore()

    def greet(step, carry):
        pl.semaphore_signal(barrier, inc=1, device_id={"tiles": lax.rem(me + step, n)})
        return carry

    lax.fori_loop(1, n, greet, 0)

    loads = [
        pltpu.make_async_copy(source, target, insem.at[place])
        for place, (source, target) in enumerate(
            (
                (slide_in, slide_ref),
                (mask_in, mask_ref),
                (label_in, label_ref),
                (tiles_in, tiles_ref),
                (lift_in, lift_ref),
                (class_in, class_ref),
                (field_ref, fbuf.at[me]),
            )
        )
    ]
    for load in loads:
        load.start()
    for tap in range(9):
        pltpu.make_async_copy(group_ref.at[:, tap], raw_w.at[tap], wsem.at[tap]).start()

    for load in loads:
        load.wait()
    lane = iota((1, LANES), 1)
    ids = jnp.full((1, LANES), -1.0, F32)
    for slot in range(slots):
        code = jnp.where(mask_ref[slot] > 0, slide_ref[slot], -1).astype(F32)
        ids = jnp.where(lane == slot, code, ids)
    isrc[...] = ids
    ibuf[me] = ids
    pl.semaphore_wait(barrier, n - 1)

    def send_first(step, carry):
        peer = {"tiles": lax.rem(me + step, n)}
        pltpu.make_async_remote_copy(
            field_ref, fbuf.at[me], fsend, frecv, device_id=peer
        ).start()
        pltpu.make_async_remote_copy(isrc, ibuf.at[me], isend, irecv, device_id=peer).start()
        return carry

    lax.fori_loop(1, n, send_first, 0)

    zeros_pad = jnp.zeros((row, 256), BF16)
    for freq in range(4):
        for shift in range(3):
            feat[freq, shift, 0:row, :] = zeros_pad
            feat[freq, shift, pixels + row : pixels + 2 * row, :] = zeros_pad

    lift_a[...] = jnp.zeros_like(lift_a)
    for tap in range(9):
        part = lift_ref[tap]
        l0, l1, l2 = part[0:1], part[1:2], part[2:3]
        mean = (l0 + l1 + l2) * (1.0 / 3.0)
        crossed = (CROSS * (l1 - l2), CROSS * (l2 - l0), CROSS * (l0 - l1))
        for colour, own in enumerate((l0, l1, l2)):
            at = slice(tap * 8 + colour, tap * 8 + colour + 1)
            lift_a[at, 0:128] = mean
            lift_a[at, 128:256] = own - mean
            lift_a[at, 256:384] = crossed[colour]
    lift_high, lift_low = split(lift_a[...])

    def prepare(tap, carry):
        pltpu.make_async_copy(group_ref.at[:, tap], raw_w.at[tap], wsem.at[tap]).wait()
        for start in range(0, 128, 32):
            x = [raw_w[tap, hue, start : start + 32, :].astype(F32) for hue in range(8)]
            parts = hue_transform(x)
            top, bottom = slice(start, start + 32), slice(128 + start, 160 + start)
            nothing = jnp.zeros((32, 128), BF16)
            wts[0, tap, top, 0:128] = (parts[0][0] * 0.125).astype(BF16)
            wts[0, tap, top, 128:256] = nothing
            wts[0, tap, bottom, 0:128] = nothing
            wts[0, tap, bottom, 128:256] = (parts[0][1] * 0.125).astype(BF16)
            for freq in range(1, 4):
                p = (parts[freq][0] * 0.25).astype(BF16)
                q = (parts[freq][1] * 0.25).astype(BF16)
                wts[freq, tap, top, 0:128] = p
                wts[freq, tap, top, 128:256] = -q
                wts[freq, tap, bottom, 0:128] = q
                wts[freq, tap, bottom, 128:256] = p
        return carry

    lax.fori_loop(0, 9, prepare, 0)

    row_slot = iota((row, classes), 0) // 8
    label_col = jnp.full((row, classes), -1, jnp.int32)
    live_col = jnp.zeros((row, classes), F32)
    for slot in range(slots):
        label_col = jnp.where(row_slot == slot, label_ref[slot], label_col)
        live_col = jnp.where(row_slot == slot, mask_ref[slot].astype(F32), live_col)
    hot = (label_col == iota((row, classes), 1)).astype(F32)
    score_grad = PIX * live_col * (1.0 / classes - hot)
    spread = lax.dot_general(
        score_grad,
        class_ref[...],
        (((1,), (0,)), ((), ())),
        precision=HIGHEST,
        preferred_element_type=F32,
    ) * (1.0 / 512.0)

    src = iota((pixels, pixels), 0)
    dst = iota((pixels, pixels), 1)
    moved = (dst // 8) % slots * PIX + dst // row * 8 + dst % 8
    permute = (src == moved).astype(F32)

    pltpu.make_async_copy(fbuf.at[pl.ds(0, n - 1)], fbuf.at[pl.ds(0, n - 1)], frecv).wait()
    halves = []
    for slot in range(slots):
        slide = slide_ref[slot]
        owner = slide // slides_own
        local = slide - owner * slides_own
        own_row = local // 2
        odd = (local - 2 * own_row).astype(F32)
        found = fbuf[owner, pl.ds(own_row, 1), :]
        turned = pltpu.roll(found, 64, 1)
        if slot % 2:
            odd = 1.0 - odd
        halves.append(found * (1.0 - odd) + turned * odd)
    angle_row = jnp.concatenate(
        [jnp.where(lane < 64, halves[i], halves[i + 1]) for i in range(0, slots, 2)], axis=1
    )
    sub = iota((8, pixels), 0)
    colours = tiles_ref[...].astype(F32)
    inputs = jnp.where(sub == 3, angle_row, 0.0)
    for colour in range(3):
        inputs = jnp.where(sub == colour, colours[colour : colour + 1], inputs)
    inputs = jnp.dot(inputs, permute, precision=HIGHEST, preferred_element_type=F32)
    red, green, blue = inputs[0:1], inputs[1:2], inputs[2:3]
    cos_angle, sin_angle = jnp.cos(inputs[3:4]), jnp.sin(inputs[3:4])
    grey = (red + green + blue) * (1.0 / 3.0)

    def stack3(rows):
        result = jnp.where(sub == 0, rows[0], 0.0)
        result = jnp.where(sub == 1, rows[1], result)
        return jnp.where(sub == 2, rows[2], result)

    crosses = (CROSS * (blue - green), CROSS * (red - blue), CROSS * (green - red))
    attacked = stack3(
        [
            cos_angle * x + sin_angle * y + (1.0 - cos_angle) * grey
            for x, y in zip((red, green, blue), crosses)
        ]
    )
    turning = stack3(
        [
            -sin_angle * x + cos_angle * y + sin_angle * grey
            for x, y in zip((red, green, blue), crosses)
        ]
    )
    lanes = iota((8, pixels), 1)
    lane_y, lane_x = lanes // row, lanes % 8

    def moved_by(value, dy, dx):
        distance = dy * row + dx
        if distance:
            value = pltpu.roll(value, (-distance) % pixels, 1)
        inside = (lane_y + dy >= 0) & (lane_y + dy < 8) & (lane_x + dx >= 0) & (lane_x + dx < 8)
        return jnp.where(inside, value, 0.0)

    patches = jnp.concatenate(
        [moved_by(attacked, dy, dx) for dy, dx in TAPS] + [jnp.zeros((8, pixels), F32)], axis=0
    )
    patch_high, patch_low = split(patches)
    base[...] = lax.dot_general(
        jnp.concatenate([patch_high, patch_low, patch_high], axis=0),
        jnp.concatenate([lift_high, lift_high, lift_low], axis=0),
        (((0,), (0,)), ((), ())),
        preferred_element_type=F32,
    )

    first = iota((slots, 8, 128), 1) == 0
    last = iota((slots, 8, 128), 1) == 7

    def put(y, values):
        at = pl.ds(pl.multiple_of(row + y * row, row), row)
        for freq, pair in enumerate(hue_transform(values)):
            for side, value in enumerate(pair):
                cols = slice(128 * side, 128 * side + 128)
                block = value.reshape(slots, 8, 128)
                left = jnp.where(first, 0.0, pltpu.roll(block, 1, 1)).reshape(row, 128)
                right = jnp.where(last, 0.0, pltpu.roll(block, 7, 1)).reshape(row, 128)
                feat[freq, 0, at, cols] = left.astype(BF16)
                feat[freq, 1, at, cols] = value.astype(BF16)
                feat[freq, 2, at, cols] = right.astype(BF16)

    def convolve(forward):
        def one(step, carry):
            totals = [jnp.zeros((pixels, 256), F32) for _ in range(2)]
            for tap, (dy, dx) in enumerate(TAPS):
                if not forward:
                    dy, dx = -dy, -dx
                start = (dy + 1) * row
                for half in range(2):
                    freq = 2 * step + half
                    totals[half] = totals[half] + lax.dot_general(
                        feat[freq, dx + 1, start : start + pixels, :],
                        wts[freq, tap],
                        (((1,), (0 if forward else 1,)), ((), ())),
                        preferred_element_type=F32,
                    )
            for half in range(2):
                prod[2 * step + half] = totals[half]
            return carry

        lax.fori_loop(0, 2, one, 0)

    def take(at):
        return hue_spread([(prod[f, at, 0:128], prod[f, at, 128:256]) for f in range(4)])

    def activate(y, carry):
        at = pl.ds(pl.multiple_of(y * row, row), row)
        b0, bc, bs = base[at, 0:128], base[at, 128:256], base[at, 256:384]
        d1 = ROOT_HALF * (bc - bs)
        d3 = ROOT_HALF * (bc + bs)
        lifted = [b0 + bc, b0 + d1, b0 - bs, b0 - d3, b0 - bc, b0 - d1, b0 + bs, b0 + d3]
        acts = []
        for hue, v in enumerate(lifted):
            g = sigmoid(v)
            act = v * g
            slope[hue, at, :] = g + act * (1.0 - g)
            acts.append(act)
        put(y, acts)
        return carry

    lax.fori_loop(0, 8, activate, 0)
    convolve(True)

    def middle(y, pooled):
        at = pl.ds(pl.multiple_of(y * row, row), row)
        grads = []
        for v in take(at):
            g = sigmoid(v)
            act = v * g
            pooled = pooled + act
            grads.append(spread * (g + act * (1.0 - g)))
        put(y, grads)
        return pooled

    pooled = lax.fori_loop(0, 8, middle, jnp.zeros((row, 128), F32))
    convolve(False)

    def finish(y, carry):
        at = pl.ds(pl.multiple_of(y * row, row), row)
        grads = [grad * slope[hue, at, :] for hue, grad in enumerate(take(at))]
        parts = hue_transform(grads)
        for place, value in enumerate((parts[0][0], parts[1][0], -parts[1][1])):
            cols = slice(128 * place, 128 * place + 128)
            high, low = split(value)
            lgrad[0, at, cols] = high
            lgrad[1, at, cols] = low
        return carry

    lax.fori_loop(0, 8, finish, 0)

    nt = (((1,), (1,)), ((), ()))
    both = lax.dot_general(
        jnp.concatenate([lift_high, lift_low], axis=0), lgrad[0], nt, preferred_element_type=F32
    )
    patch_grad = (
        both[0:80] + both[80:160]
        + lax.dot_general(lift_high, lgrad[1], nt, preferred_element_type=F32)
    )
    colour_grad = jnp.zeros((8, pixels), F32)
    for tap, (dy, dx) in enumerate(TAPS):
        colour_grad = colour_grad + moved_by(patch_grad[tap * 8 : tap * 8 + 8], -dy, -dx)
    angle_grad = jnp.sum(colour_grad * turning, axis=0, keepdims=True)
    by_slot = jnp.where((lanes // 8) % slots // 2 == sub, angle_grad, 0.0)
    pick_src = iota((pixels, 128), 0)
    pick_lane = iota((pixels, 128), 1)
    pick_slot = pick_src // 8 % slots
    pick = (pick_src // row * 8 + pick_src % 8 + pick_slot % 2 * 64 == pick_lane).astype(F32)
    grads = jnp.dot(by_slot, pick, precision=HIGHEST, preferred_element_type=F32)
    gsrc[...] = grads
    gbuf[me] = grads

    def send_second(step, carry):
        peer = {"tiles": lax.rem(me + step, n)}
        pltpu.make_async_remote_copy(
            gsrc.at[0:pairs], gbuf.at[me, 0:pairs], gsend, grecv, device_id=peer
        ).start()
        return carry

    lax.fori_loop(1, n, send_second, 0)

    scored = pooled * spread
    for slot in range(slots):
        margins_ref[slot] = -jnp.sum(scored[8 * slot : 8 * slot + 8]) * (1.0 / PIX)

    others = pl.ds(0, n - 1)
    pltpu.make_async_copy(ibuf.at[others], ibuf.at[others], irecv).wait()
    codes = jnp.broadcast_to(ibuf[...], (n, 8, LANES)).reshape(n * 8, LANES)
    place, col = iota((n * 8, LANES), 0) % 8, iota((n * 8, LANES), 1)
    wanted = jnp.where(col < 64, 2 * col, 2 * (col - 64) + 1)
    wanted = jnp.where(col % 64 < rows_own, wanted + me * slides_own, -2).astype(F32)
    choosers = []
    for side in range(2):
        code = jnp.sum(jnp.where(col == 2 * place + side, codes, 0.0), axis=1, keepdims=True)
        chosen = ((code == wanted) & (place < pairs)).astype(F32)
        choosers.append(chosen.T.astype(BF16))
    ones = jnp.ones((n * 8, LANES), BF16)
    counts = jnp.dot(choosers[0], ones, preferred_element_type=F32)
    counts = counts + jnp.dot(choosers[1], ones, preferred_element_type=F32)
    weight = 1.0 / jnp.maximum(counts, 1.0)
    chooser = jnp.concatenate(choosers * 2, axis=1)

    pltpu.make_async_copy(gbuf.at[others, 0:pairs], gbuf.at[others, 0:pairs], grecv).wait()
    gathered = gbuf[...].reshape(n * 8, LANES)
    high, low = split(gathered)
    high_turned, low_turned = split(pltpu.roll(gathered, 64, 1))
    sums = weight * jnp.dot(
        chooser,
        jnp.concatenate([high, high_turned, low, low_turned], axis=0),
        preferred_element_type=F32,
    )
    left = iota((64, LANES), 1) < 64
    out_ref[...] = jnp.where(left, sums[0:64], pltpu.roll(sums[64:128], 64, 1))[0:rows_own]

    pltpu.make_async_copy(fbuf.at[others], fbuf.at[others], fsend).wait()
    pltpu.make_async_copy(ibuf.at[others], ibuf.at[others], isend).wait()
    pltpu.make_async_copy(gbuf.at[others, 0:pairs], gbuf.at[others, 0:pairs], gsend).wait()


def publish(margins_in, grads_in, margins_out, grads_out, margins_mid, grads_mid, sem):
    first = pltpu.make_async_copy(margins_in, margins_mid, sem.at[0])
    second = pltpu.make_async_copy(grads_in, grads_mid, sem.at[1])
    first.start()
    second.start()
    first.wait()
    third = pltpu.make_async_copy(margins_mid, margins_out, sem.at[0])
    third.start()
    second.wait()
    fourth = pltpu.make_async_copy(grads_mid, grads_out, sem.at[1])
    fourth.start()
    third.wait()
    fourth.wait()


def solution(mesh):
    n = mesh.shape["tiles"]

    def shards(tiles, slide, mask, label, field, lift_weight, group_weight, class_weight):
        slots = slide.shape[0]
        rows_own = field.shape[0] // LANES
        pixels = slots * PIX
        vmem = pl.BlockSpec(memory_space=pltpu.VMEM)
        smem = pl.BlockSpec(memory_space=pltpu.SMEM)
        margins, grads = pl.pallas_call(
            functools.partial(kernel, n, slots, rows_own),
            out_shape=(
                jax.ShapeDtypeStruct((slots,), F32),
                jax.ShapeDtypeStruct((rows_own, LANES), F32),
            ),
            in_specs=[pl.BlockSpec(memory_space=pltpu.HBM)] * 8,
            out_specs=(smem, vmem),
            scratch_shapes=[
                pltpu.SMEM((slots,), jnp.int32),
                pltpu.SMEM((slots,), jnp.int32),
                pltpu.SMEM((slots,), jnp.int32),
                pltpu.VMEM((3, pixels), BF16),
                pltpu.VMEM(lift_weight.shape, F32),
                pltpu.VMEM(class_weight.shape[::-1], F32),
                pltpu.VMEM((9, 8, 128, 128), BF16),
                pltpu.VMEM((4, 9, 256, 256), BF16),
                pltpu.VMEM((4, 3, pixels + 16 * slots, 256), BF16),
                pltpu.VMEM((4, pixels, 256), F32),
                pltpu.VMEM((8, pixels, 128), F32),
                pltpu.VMEM((80, 384), F32),
                pltpu.VMEM((pixels, 384), F32),
                pltpu.VMEM((2, pixels, 384), BF16),
                pltpu.VMEM((n, rows_own, LANES), F32),
                pltpu.VMEM((1, LANES), F32),
                pltpu.VMEM((n, 1, LANES), F32),
                pltpu.VMEM((8, LANES), F32),
                pltpu.VMEM((n, 8, LANES), F32),
                pltpu.SemaphoreType.DMA((7,)),
                pltpu.SemaphoreType.DMA((9,)),
            ]
            + [pltpu.SemaphoreType.DMA] * 6,
            compiler_params=pltpu.CompilerParams(
                collective_id=0, has_side_effects=True, vmem_limit_bytes=66_950_000
            ),
        )(
            slide,
            mask,
            label,
            tiles,
            field.reshape(rows_own, LANES),
            lift_weight,
            group_weight,
            class_weight.T,
        )
        hbm = pl.BlockSpec(memory_space=pltpu.HBM)
        margins, grads = pl.pallas_call(
            publish,
            out_shape=(
                jax.ShapeDtypeStruct((slots,), F32),
                jax.ShapeDtypeStruct((rows_own, LANES), F32),
            ),
            in_specs=[hbm, hbm],
            out_specs=(hbm, hbm),
            scratch_shapes=[
                pltpu.SMEM((slots,), F32),
                pltpu.VMEM((rows_own, LANES), F32),
                pltpu.SemaphoreType.DMA((2,)),
            ],
            compiler_params=pltpu.CompilerParams(vmem_limit_bytes=66_950_000),
        )(margins, grads)
        return margins, grads.reshape(-1)

    split_all = P(("groups", "tiles"))
    return jax.shard_map(
        shards,
        mesh=mesh,
        in_specs=(
            P(None, ("groups", "tiles")),
            split_all,
            split_all,
            split_all,
            split_all,
            P(),
            P(),
            P(),
        ),
        out_specs=(split_all, split_all),
        check_vma=False,
    )
```
